1024 devices in a mesh: ctx: 64 (over x_hi, z), ch: 16 (over y, x_lo, core).
Axes of the slice: x: 4 (x_hi: 2, x_lo: 2; x = x_hi * 2 + x_lo), y: 4, z: 32, core: 2. Of those that a mesh axis runs over, the one named last changes fastest.
Arguments:
- inputs: bfloat16 [1536, 131072], P('ch', 'ctx'), may hold values from -6 to 6
- conv_weight: bfloat16 [3, 1536, 96], replicated, may hold values from -0.375 to 0.375
- pw_weight: bfloat16 [1536, 1536], replicated, may hold values from -0.15625 to 0.15625
- cotangent: bfloat16 [1536, 131072], P(None, ('ctx', 'ch')), may hold values from -6 to 6
Outputs:
- mixed: bfloat16 [1536, 131072], P(None, ('ctx', 'ch'))
- grad_inputs: bfloat16 [1536, 131072], P('ch', 'ctx')
The draws below stay inside these ranges and needn't reach their ends.
All inputs are finite; a program needn't handle non-finite values.
Results may differ from the reference program's by a relative error of at most 0.012.
Values may be sent and summed in bfloat16 or wider, within the bound.
A program may use at most 32 MiB of HBM per device.

```python
import jax
import jax.numpy as jnp
from jax import lax

CHANNELS = 1536
GROUP = 96
DILATION_STEP = 512
POSITIONS_EACH = 2048
SEQ = 131072
N_CTX = 64


def block_levels(rng, extent, shards, least, top_value):
    gain, own = 1.0, jax.random.fold_in(rng, 6)
    for axis_at, blocks in shards:
        heights = jnp.exp(jax.random.uniform(jax.random.fold_in(own, axis_at), (blocks,), jnp.float32, least / len(shards), top_value / len(shards)))
        gain = gain * jnp.repeat(heights, extent[axis_at] // blocks).reshape([-1 if axis == axis_at else 1 for axis in range(len(extent))])
    return gain


def normal_values(rng, shape, scale, bound, shards=(), held_as=jnp.bfloat16):
    values = jax.random.normal(rng, shape, jnp.float32) * scale
    if len(shards) > 0:
        values = block_levels(rng, shape, shards, -0.22, 0.18) * values
    return jnp.clip(values, min=-bound, max=bound).astype(held_as)


def setup_inputs(seed: int = 0) -> dict:
    seeds = jax.random.split(jax.random.key(seed), 5)
    inputs = normal_values(seeds[0], (CHANNELS, SEQ), 1.0, 6.0, ((0, 16), (1, 64)))
    conv_weight = normal_values(seeds[1], (3, CHANNELS, GROUP), (3 * GROUP) ** -0.5, 0.375)
    pw_weight = normal_values(seeds[2], (CHANNELS, CHANNELS), CHANNELS ** -0.5, 0.15625)
    cotangent = normal_values(seeds[3], (CHANNELS, SEQ), 1.0, 6.0, ((1, 1024),))
    return {"inputs": inputs, "conv_weight": conv_weight, "pw_weight": pw_weight, "cotangent": cotangent}


def gelu_slope(values):
    return jax.vjp(jax.nn.gelu, values)[1](jnp.ones_like(values))[0]

def group_conv(kernel_taps, conv_weight):
    channels, length = kernel_taps[0].shape
    width = conv_weight.shape[2]
    groups = channels // width
    total = jnp.zeros((groups, width, length), jnp.float32)
    for position_offset in range(3):
        kernel = conv_weight[position_offset].reshape(groups, width, width).astype(jnp.float32)
        signal = kernel_taps[position_offset].reshape(groups, width, length).astype(jnp.float32)
        total = total + jnp.einsum('gji,gip->gjp', kernel, signal)
    return total.reshape(channels, length)

def group_conv_back(kernel_taps, conv_weight):
    channels, length = kernel_taps[0].shape
    width = conv_weight.shape[2]
    groups = channels // width
    total = jnp.zeros((groups, width, length), jnp.float32)
    for position_offset in range(3):
        kernel = conv_weight[position_offset].reshape(groups, width, width).astype(jnp.float32)
        signal = kernel_taps[position_offset].reshape(groups, width, length).astype(jnp.float32)
        total = total + jnp.einsum('gji,gjp->gip', kernel, signal)
    return total.reshape(channels, length)

def joined_edges(stack):
    return jnp.moveaxis(stack, 0, 1).reshape(stack.shape[1], stack.shape[0] * stack.shape[2])

def reference(inputs, conv_weight, pw_weight, cotangent):
    widened_input = jnp.pad(inputs, ((0, 0), (DILATION_STEP, DILATION_STEP)))
    blocks = jnp.arange(N_CTX, dtype=jnp.int32)

    def forward_block(block):
        first_position = (block * POSITIONS_EACH).astype(jnp.int32)
        sliding_window = lax.dynamic_slice_in_dim(widened_input, first_position, POSITIONS_EACH + 2 * DILATION_STEP, 1)
        kernel_taps = [sliding_window[:, position_offset * DILATION_STEP:position_offset * DILATION_STEP + POSITIONS_EACH] for position_offset in range(3)]
        conv_out = group_conv(kernel_taps, conv_weight)
        active = jax.nn.gelu(conv_out).astype(jnp.bfloat16)
        mixed = jnp.dot(pw_weight, active, preferred_element_type=jnp.float32).astype(jnp.bfloat16)
        upstream = lax.dynamic_slice_in_dim(cotangent, first_position, POSITIONS_EACH, 1)
        grad_active = lax.dot_general(pw_weight, upstream, (((0,), (0,)), ((), ())), preferred_element_type=jnp.float32).astype(jnp.bfloat16)
        convolved_gradient = (grad_active.astype(jnp.float32) * gelu_slope(conv_out)).astype(jnp.bfloat16)
        return (mixed, convolved_gradient)
    mixed, convolved_gradient = lax.map(forward_block, blocks)
    mixed = joined_edges(mixed)
    gradient_widened = jnp.pad(joined_edges(convolved_gradient), ((0, 0), (DILATION_STEP, DILATION_STEP)))

    def backward_block(block):
        first_position = (block * POSITIONS_EACH).astype(jnp.int32)
        sliding_window = lax.dynamic_slice_in_dim(gradient_widened, first_position, POSITIONS_EACH + 2 * DILATION_STEP, 1)
        kernel_taps = [sliding_window[:, (2 - position_offset) * DILATION_STEP:(2 - position_offset) * DILATION_STEP + POSITIONS_EACH] for position_offset in range(3)]
        return group_conv_back(kernel_taps, conv_weight).astype(jnp.bfloat16)
    grad_inputs = joined_edges(lax.map(backward_block, blocks))
    return (mixed, grad_inputs)
```

```python
import functools

import jax
import jax.numpy as jnp
from jax import lax
from jax.experimental import pallas as pl
from jax.experimental.pallas import tpu as pltpu
from jax.sharding import PartitionSpec as P

STEP = 512
TAPS = 3
CUBIC = 0.044715
SCALE = 0.7978845608028654
NT = (((1,), (1,)), ((), ()))


def gelu_and_slope(v):
    square = v * v
    t = jnp.tanh(SCALE * v * (1.0 + CUBIC * square))
    half = 0.5 * (1.0 + t)
    slope = half + 0.5 * v * (1.0 - t * t) * (SCALE * (1.0 + 3.0 * CUBIC * square))
    return v * half, slope


def kernel(
    n_ctx, x_hbm, wt_hbm, pw_hbm, cot_hbm, mixed_ref, gin_ref,
    xc, gc, wwin, pw_v, cot_v, cot_t, slope, act_send, act_recv, ga_send, ga_recv, total,
    load_sem, halo_send, halo_recv, act_ssem, act_rsem, ga_ssem, ga_rsem,
):
    width, block = act_send.shape[1:]
    quads = 4
    me_ctx, me = lax.axis_index("ctx"), lax.axis_index("ch")
    y, x, core = me // 4, (me // 2) % 2, me % 2
    wide = quads * width

    barrier = pltpu.get_barrier_semaphore()
    for k in range(1, 16):
        pl.semaphore_signal(barrier, inc=1, device_id={"ch": lax.rem(me + k, 16)})

    @pl.when(me_ctx > 0)
    def _():
        pl.semaphore_signal(barrier, inc=1, device_id={"ctx": me_ctx - 1})

    @pl.when(me_ctx < n_ctx - 1)
    def _():
        pl.semaphore_signal(barrier, inc=1, device_id={"ctx": me_ctx + 1})

    start = jnp.minimum((width * me) // 128, (16 * width) // 128 - 2) * 128
    off = width * me - start
    w_load = pltpu.make_async_copy(
        wt_hbm.at[:, :, pl.ds(pl.multiple_of(start, 128), 256)], wwin, load_sem.at[0]
    )
    w_load.start()
    x_loads = []
    for q in range(4):
        x_loads.append(
            pltpu.make_async_copy(x_hbm.at[:, pl.ds(STEP * q, STEP)], xc.at[q + 1], load_sem.at[1 + q])
        )
        x_loads[-1].start()
    cot_load = pltpu.make_async_copy(cot_hbm, cot_v, load_sem.at[5])
    cot_load.start()
    order = (1, 3, 2, 0)
    pw_loads = []
    for n, dy in enumerate(order):
        at = pl.multiple_of(lax.rem(y + dy, 4) * wide, 128)
        pw_loads.append(
            pltpu.make_async_copy(pw_hbm.at[:, pl.ds(at, wide)], pw_v.at[n], load_sem.at[6 + n])
        )
        pw_loads[-1].start()

    w_load.wait()
    rows = lax.broadcasted_iota(jnp.int32, (width, 256), 0)
    lanes = lax.broadcasted_iota(jnp.int32, (width, 256), 1)
    pick = jnp.where(lanes == rows + off, 1.0, 0.0).astype(jnp.bfloat16)
    w_cat = lax.dot_general(
        pick, wwin[...].reshape(TAPS * width, 256), NT, preferred_element_type=jnp.float32
    ).astype(jnp.bfloat16)
    depth = lax.broadcasted_iota(jnp.int32, (256, TAPS * width), 0)
    column = lax.broadcasted_iota(jnp.int32, (256, TAPS * width), 1)
    wt_cat = jnp.zeros((width, TAPS * width), jnp.float32)
    for t in range(TAPS):
        hit = (depth == column - width * t + off) & (column >= width * t) & (column < width * (t + 1))
        place = jnp.where(hit, 1.0, 0.0).astype(jnp.bfloat16)
        wt_cat = wt_cat + jnp.dot(wwin[t], place, preferred_element_type=jnp.float32)
    wt_cat = wt_cat.astype(jnp.bfloat16)

    def conv(q):
        signal = jnp.concatenate([xc[q], xc[q + 1], xc[q + 2]], axis=0)
        act, tilt = gelu_and_slope(jnp.dot(w_cat, signal, preferred_element_type=jnp.float32))
        slope[q] = tilt
        act = act.astype(jnp.bfloat16)
        for b in range(4):
            act_send[4 * q + b] = act[:, block * b : block * (b + 1)]

    def send_act(q):
        for n, (dx, dc) in enumerate(((1, 0), (1, 1), (0, 1), (0, 0))):
            to = 4 * q + 2 * lax.rem(x + dx, 2) + lax.rem(core + dc, 2)
            copy = pltpu.make_async_remote_copy(
                src_ref=act_send.at[to],
                dst_ref=act_recv.at[pl.ds(pl.multiple_of(width * me, width), width), :],
                send_sem=act_ssem.at[4 * q + n],
                recv_sem=act_rsem.at[me],
                device_id={"ch": to},
            )
            if dx or dc:
                copy.start()
            else:
                pl.when(y != q)(copy.start)

                @pl.when(y == q)
                def _():
                    pltpu.make_async_copy(
                        act_send.at[to],
                        act_recv.at[pl.ds(pl.multiple_of(width * me, width), width), :],
                        act_rsem.at[me],
                    ).start()

    def wait_sent(q_sems, buffer):
        pltpu.make_async_copy(buffer, buffer, q_sems).wait()

    for q in range(4):
        x_loads[q].wait()
    conv(1)
    conv(2)

    pl.semaphore_wait(barrier, 15 + (me_ctx > 0).astype(jnp.int32) + (me_ctx < n_ctx - 1).astype(jnp.int32))

    def halo(buffer, side, base):
        return pltpu.make_async_remote_copy(
            src_ref=buffer.at[1 if side == 0 else 4],
            dst_ref=buffer.at[5 if side == 0 else 0],
            send_sem=halo_send.at[base + side],
            recv_sem=halo_recv.at[base + side],
            device_id={"ctx": me_ctx - 1 if side == 0 else me_ctx + 1},
        )

    has_left, has_right = me_ctx > 0, me_ctx < n_ctx - 1
    pl.when(has_left)(lambda: halo(xc, 0, 0).start())
    pl.when(has_right)(lambda: halo(xc, 1, 0).start())
    send_act(1)
    send_act(2)

    cot_load.wait()
    cot_t[...] = cot_v[...].T
    for n, dy in enumerate(order):
        pw_loads[n].wait()
        part = jnp.dot(cot_t[...], pw_v[n], preferred_element_type=jnp.float32)
        to_y = lax.rem(y + dy, 4)
        flipped = part.T.astype(jnp.bfloat16)
        for b in range(4):
            ga_send[4 * n + b] = flipped[width * b : width * (b + 1), :]
        for k, (dx, dc) in enumerate(((1, 0), (1, 1), (0, 1), (0, 0))):
            low = 2 * lax.rem(x + dx, 2) + lax.rem(core + dc, 2)
            if dy or dx or dc:
                pltpu.make_async_remote_copy(
                    src_ref=ga_send.at[4 * n + low],
                    dst_ref=ga_recv.at[me],
                    send_sem=ga_ssem.at[4 * n + k],
                    recv_sem=ga_rsem.at[me],
                    device_id={"ch": 4 * to_y + low},
                ).start()
            else:
                pltpu.make_async_copy(ga_send.at[4 * n + low], ga_recv.at[me], ga_rsem.at[me]).start()

    @pl.when(has_left)
    def _():
        halo(xc, 1, 0).wait_recv()

    @pl.when(jnp.logical_not(has_left))
    def _():
        xc[0] = jnp.zeros(xc.shape[1:], xc.dtype)

    conv(0)
    send_act(0)

    @pl.when(has_right)
    def _():
        halo(xc, 0, 0).wait_recv()

    @pl.when(jnp.logical_not(has_right))
    def _():
        xc[5] = jnp.zeros(xc.shape[1:], xc.dtype)

    conv(3)
    send_act(3)

    def grad_conv(q):
        for b in range(4):
            s = 4 * q + b
            pltpu.make_async_copy(ga_recv.at[s], ga_recv.at[s], ga_rsem.at[s]).wait()
            gc[q + 1, :, pl.ds(block * b, block)] = (
                ga_recv[s].astype(jnp.float32) * slope[q, :, pl.ds(block * b, block)]
            ).astype(jnp.bfloat16)

    grad_conv(0)
    pl.when(has_left)(lambda: halo(gc, 0, 2).start())
    grad_conv(3)
    pl.when(has_right)(lambda: halo(gc, 1, 2).start())
    grad_conv(1)
    grad_conv(2)

    def back(q):
        signal = jnp.concatenate([gc[q + 2], gc[q + 1], gc[q]], axis=0)
        gin_ref[:, pl.ds(STEP * q, STEP)] = jnp.dot(
            wt_cat, signal, preferred_element_type=jnp.float32
        ).astype(jnp.bfloat16)

    back(1)
    back(2)

    @pl.when(has_left)
    def _():
        halo(gc, 1, 2).wait_recv()

    @pl.when(jnp.logical_not(has_left))
    def _():
        gc[0] = jnp.zeros(gc.shape[1:], gc.dtype)

    back(0)

    @pl.when(has_right)
    def _():
        halo(gc, 0, 2).wait_recv()

    @pl.when(jnp.logical_not(has_right))
    def _():
        gc[5] = jnp.zeros(gc.shape[1:], gc.dtype)

    back(3)

    visit = (3, 0, 1, 2)
    for k, n in enumerate(visit):
        from_y = lax.rem(y + order[n], 4)
        for b in range(4):
            s = 4 * from_y + b
            piece = act_recv.at[pl.ds(pl.multiple_of(width * s, width), width), :]
            pltpu.make_async_copy(piece, piece, act_rsem.at[s]).wait()
        part = jnp.dot(
            pw_v[n],
            act_recv[pl.ds(pl.multiple_of(wide * from_y, wide), wide), :],
            preferred_element_type=jnp.float32,
        )
        if k == 0:
            total[...] = part
        elif k < 3:
            total[...] += part
        else:
            mixed_ref[...] = (total[...] + part).astype(jnp.bfloat16)

    for q in range(4):
        for n in range(4):
            if n < 3:
                wait_sent(act_ssem.at[4 * q + n], act_send.at[0])
            else:
                pl.when(y != q)(lambda: wait_sent(act_ssem.at[4 * q + n], act_send.at[0]))
            if order[q] or n < 3:
                wait_sent(ga_ssem.at[4 * q + n], ga_send.at[0])
    for base, buffer in ((0, xc), (2, gc)):
        pl.when(has_left)(lambda: halo(buffer, 0, base).wait_send())
        pl.when(has_right)(lambda: halo(buffer, 1, base).wait_send())


def body(n_ctx, inputs, conv_weight, pw_weight, cotangent):
    width, length = inputs.shape
    channels, block = cotangent.shape
    bf16, f32 = jnp.bfloat16, jnp.float32
    dma = pltpu.SemaphoreType.DMA
    return pl.pallas_call(
        functools.partial(kernel, n_ctx),
        out_shape=(
            jax.ShapeDtypeStruct((channels, block), bf16),
            jax.ShapeDtypeStruct((width, length), bf16),
        ),
        in_specs=[pl.BlockSpec(memory_space=pl.ANY)] * 4,
        out_specs=[pl.BlockSpec(memory_space=pltpu.VMEM)] * 2,
        scratch_shapes=[
            pltpu.VMEM((6, width, STEP), bf16),
            pltpu.VMEM((6, width, STEP), bf16),
            pltpu.VMEM((TAPS, width, 256), bf16),
            pltpu.VMEM((4, channels, 4 * width), bf16),
            pltpu.VMEM((channels, block), bf16),
            pltpu.VMEM((block, channels), bf16),
            pltpu.VMEM((4, width, STEP), f32),
            pltpu.VMEM((16, width, block), bf16),
            pltpu.VMEM((channels, block), bf16),
            pltpu.VMEM((16, width, block), bf16),
            pltpu.VMEM((16, width, block), bf16),
            pltpu.VMEM((channels, block), f32),
            dma((10,)),
            dma((4,)),
            dma((4,)),
            dma((16,)),
            dma((16,)),
            dma((16,)),
            dma((16,)),
        ],
        compiler_params=pltpu.CompilerParams(
            collective_id=0, has_side_effects=True, vmem_limit_bytes=40 * 1024 * 1024
        ),
        name="conv_mix_grad",
    )(*(
        pltpu.with_memory_space_constraint(a, pltpu.HBM)
        for a in (inputs, jnp.transpose(conv_weight, (0, 2, 1)), pw_weight, cotangent)
    ))


def solution(mesh):
    return jax.shard_map(
        functools.partial(body, mesh.shape["ctx"]),
        mesh=mesh,
        in_specs=(P("ch", "ctx"), P(), P(), P(None, ("ctx", "ch"))),
        out_specs=(P(None, ("ctx", "ch")), P("ch", "ctx")),
        check_vma=False,
    )
```

```python
import functools

import jax
import jax.numpy as jnp
from jax import lax
from jax.experimental import pallas as pl
from jax.experimental.pallas import tpu as pltpu
from jax.sharding import PartitionSpec as P

STEP = 512
TAPS = 3
CUBIC = 0.044715
SCALE = 0.7978845608028654
NT = (((1,), (1,)), ((), ()))


def gelu_and_slope(v):
    square = v * v
    t = jnp.tanh(SCALE * v * (1.0 + CUBIC * square))
    half = 0.5 * (1.0 + t)
    slope = half + 0.5 * v * (1.0 - t * t) * (SCALE * (1.0 + 3.0 * CUBIC * square))
    return v * half, slope


def kernel(
    n_ctx, x_hbm, wt_hbm, pw_hbm, cot_hbm, mixed_ref, gin_ref,
    xc, gc, wwin, pw_v, cot_v, cot_t, slope, act_send, act_recv, ga_send, ga_recv, total,
    load_sem, halo_send, halo_recv, act_ssem, act_rsem, ga_ssem, ga_rsem,
):
    width, block = act_send.shape[1:]
    quads = 4
    me_ctx, me = lax.axis_index("ctx"), lax.axis_index("ch")
    y, x, core = me // 4, (me // 2) % 2, me % 2
    wide = quads * width

    barrier = pltpu.get_barrier_semaphore()
    has_left, has_right = me_ctx > 0, me_ctx < n_ctx - 1
    seam = n_ctx // 2 - 1
    for k in range(1, 16):
        pl.semaphore_signal(barrier, inc=1, device_id={"ch": lax.rem(me + k, 16)})

    @pl.when(has_left)
    def _():
        pl.semaphore_signal(barrier, inc=1, device_id={"ctx": me_ctx - 1})

    @pl.when(has_right)
    def _():
        pl.semaphore_signal(barrier, inc=1, device_id={"ctx": me_ctx + 1})

    cot_load = pltpu.make_async_copy(cot_hbm, cot_v, load_sem.at[5])
    cot_load.start()
    order = (1, 3, 2, 0)
    pw_loads = []

    def load_pw(n):
        at = pl.multiple_of(lax.rem(y + order[n], 4) * wide, 128)
        pw_loads.append(
            pltpu.make_async_copy(pw_hbm.at[:, pl.ds(at, wide)], pw_v.at[n], load_sem.at[6 + n])
        )
        pw_loads[-1].start()

    load_pw(0)
    start = jnp.minimum((width * me) // 128, (16 * width) // 128 - 2) * 128
    off = width * me - start
    w_load = pltpu.make_async_copy(
        wt_hbm.at[:, :, pl.ds(pl.multiple_of(start, 128), 256)], wwin, load_sem.at[0]
    )
    w_load.start()
    x_loads = []
    for q in range(4):
        x_loads.append(
            pltpu.make_async_copy(x_hbm.at[:, pl.ds(STEP * q, STEP)], xc.at[q + 1], load_sem.at[1 + q])
        )
        x_loads[-1].start()
    for n in range(1, 4):
        load_pw(n)

    def halo(buffer, side, base):
        return pltpu.make_async_remote_copy(
            src_ref=buffer.at[1 if side == 0 else 4],
            dst_ref=buffer.at[5 if side == 0 else 0],
            send_sem=halo_send.at[base + side],
            recv_sem=halo_recv.at[base + side],
            device_id={"ctx": me_ctx - 1 if side == 0 else me_ctx + 1},
        )

    cot_load.wait()
    cot_t[...] = cot_v[...].T

    def grad_active(n):
        pw_loads[n].wait()
        flipped = jnp.dot(cot_t[...], pw_v[n], preferred_element_type=jnp.float32).T.astype(jnp.bfloat16)
        for b in range(4):
            ga_send[4 * n + b] = flipped[width * b : width * (b + 1), :]

    def send_ga(n):
        dy = order[n]
        for k, (dx, dc) in enumerate(((1, 0), (1, 1), (0, 1), (0, 0))):
            low = 2 * lax.rem(x + dx, 2) + lax.rem(core + dc, 2)
            if dy or dx or dc:
                pltpu.make_async_remote_copy(
                    src_ref=ga_send.at[4 * n + low],
                    dst_ref=ga_recv.at[me],
                    send_sem=ga_ssem.at[4 * n + k],
                    recv_sem=ga_rsem.at[me],
                    device_id={"ch": 4 * lax.rem(y + dy, 4) + low},
                ).start()
            else:
                pltpu.make_async_copy(ga_send.at[4 * n + low], ga_recv.at[me], ga_rsem.at[me]).start()

    grad_active(0)
    for q in range(4):
        x_loads[q].wait()
    pl.semaphore_wait(barrier, 15 + has_left.astype(jnp.int32) + has_right.astype(jnp.int32))
    pl.when(has_right)(lambda: halo(xc, 1, 0).start())
    pl.when(has_left)(lambda: halo(xc, 0, 0).start())
    send_ga(0)
    for n in range(1, 4):
        grad_active(n)
        send_ga(n)

    w_load.wait()
    rows = lax.broadcasted_iota(jnp.int32, (width, 256), 0)
    lanes = lax.broadcasted_iota(jnp.int32, (width, 256), 1)
    pick = jnp.where(lanes == rows + off, 1.0, 0.0).astype(jnp.bfloat16)
    w_cat = lax.dot_general(
        pick, wwin[...].reshape(TAPS * width, 256), NT, preferred_element_type=jnp.float32
    ).astype(jnp.bfloat16)
    depth = lax.broadcasted_iota(jnp.int32, (256, TAPS * width), 0)
    column = lax.broadcasted_iota(jnp.int32, (256, TAPS * width), 1)
    wt_cat = jnp.zeros((width, TAPS * width), jnp.float32)
    for t in range(TAPS):
        hit = (depth == column - width * t + off) & (column >= width * t) & (column < width * (t + 1))
        place = jnp.where(hit, 1.0, 0.0).astype(jnp.bfloat16)
        wt_cat = wt_cat + jnp.dot(wwin[t], place, preferred_element_type=jnp.float32)
    wt_cat = wt_cat.astype(jnp.bfloat16)

    def conv(q):
        signal = jnp.concatenate([xc[q], xc[q + 1], xc[q + 2]], axis=0)
        act, tilt = gelu_and_slope(jnp.dot(w_cat, signal, preferred_element_type=jnp.float32))
        slope[q] = tilt
        act = act.astype(jnp.bfloat16)
        for b in range(4):
            act_send[4 * q + b] = act[:, block * b : block * (b + 1)]

    def send_act(q):
        for n, (dx, dc) in enumerate(((1, 0), (1, 1), (0, 1), (0, 0))):
            to = 4 * q + 2 * lax.rem(x + dx, 2) + lax.rem(core + dc, 2)
            copy = pltpu.make_async_remote_copy(
                src_ref=act_send.at[to],
                dst_ref=act_recv.at[pl.ds(pl.multiple_of(width * me, width), width), :],
                send_sem=act_ssem.at[4 * q + n],
                recv_sem=act_rsem.at[me],
                device_id={"ch": to},
            )
            if dx or dc:
                copy.start()
            else:
                pl.when(y != q)(copy.start)

                @pl.when(y == q)
                def _():
                    pltpu.make_async_copy(
                        act_send.at[to],
                        act_recv.at[pl.ds(pl.multiple_of(width * me, width), width), :],
                        act_rsem.at[me],
                    ).start()

    def wait_sent(q_sems, buffer):
        pltpu.make_async_copy(buffer, buffer, q_sems).wait()

    conv(1)
    send_act(1)
    conv(2)
    send_act(2)

    @pl.when(has_left)
    def _():
        halo(xc, 1, 0).wait_recv()

    @pl.when(jnp.logical_not(has_left))
    def _():
        xc[0] = jnp.zeros(xc.shape[1:], xc.dtype)

    conv(0)
    pl.when(me_ctx != seam)(lambda: send_act(0))

    @pl.when(has_right)
    def _():
        halo(xc, 0, 0).wait_recv()

    @pl.when(jnp.logical_not(has_right))
    def _():
        xc[5] = jnp.zeros(xc.shape[1:], xc.dtype)

    conv(3)
    pl.when(me_ctx != seam)(lambda: send_act(3))

    def grad_conv(q):
        for b in range(4):
            s = 4 * q + b
            pltpu.make_async_copy(ga_recv.at[s], ga_recv.at[s], ga_rsem.at[s]).wait()
            gc[q + 1, :, pl.ds(block * b, block)] = (
                ga_recv[s].astype(jnp.float32) * slope[q, :, pl.ds(block * b, block)]
            ).astype(jnp.bfloat16)

    grad_conv(3)
    pl.when(has_right)(lambda: halo(gc, 1, 2).start())
    grad_conv(0)
    pl.when(has_left)(lambda: halo(gc, 0, 2).start())

    @pl.when(me_ctx == seam)
    def _():
        send_act(0)
        send_act(3)

    grad_conv(1)
    grad_conv(2)

    def back(q):
        signal = jnp.concatenate([gc[q + 2], gc[q + 1], gc[q]], axis=0)
        gin_ref[:, pl.ds(STEP * q, STEP)] = jnp.dot(
            wt_cat, signal, preferred_element_type=jnp.float32
        ).astype(jnp.bfloat16)

    back(1)
    back(2)

    visit = (3, 0, 1, 2)

    def mix(k):
        n = visit[k]
        from_y = lax.rem(y + order[n], 4)
        for b in range(4):
            s = 4 * from_y + b
            piece = act_recv.at[pl.ds(pl.multiple_of(width * s, width), width), :]
            pltpu.make_async_copy(piece, piece, act_rsem.at[s]).wait()
        part = jnp.dot(
            pw_v[n],
            act_recv[pl.ds(pl.multiple_of(wide * from_y, wide), wide), :],
            preferred_element_type=jnp.float32,
        )
        if k == 0:
            total[...] = part
        elif k < 3:
            total[...] += part
        else:
            mixed_ref[...] = (total[...] + part).astype(jnp.bfloat16)

    for k in range(3):
        mix(k)

    @pl.when(has_right)
    def _():
        halo(gc, 0, 2).wait_recv()

    @pl.when(jnp.logical_not(has_right))
    def _():
        gc[5] = jnp.zeros(gc.shape[1:], gc.dtype)

    back(3)
    mix(3)

    @pl.when(has_left)
    def _():
        halo(gc, 1, 2).wait_recv()

    @pl.when(jnp.logical_not(has_left))
    def _():
        gc[0] = jnp.zeros(gc.shape[1:], gc.dtype)

    back(0)

    for q in range(4):
        for n in range(4):
            if n < 3:
                wait_sent(act_ssem.at[4 * q + n], act_send.at[0])
            else:
                pl.when(y != q)(lambda: wait_sent(act_ssem.at[4 * q + n], act_send.at[0]))
            if order[q] or n < 3:
                wait_sent(ga_ssem.at[4 * q + n], ga_send.at[0])
    for base, buffer in ((0, xc), (2, gc)):
        pl.when(has_left)(lambda: halo(buffer, 0, base).wait_send())
        pl.when(has_right)(lambda: halo(buffer, 1, base).wait_send())


def body(n_ctx, inputs, conv_weight, pw_weight, cotangent):
    width, length = inputs.shape
    channels, block = cotangent.shape
    bf16, f32 = jnp.bfloat16, jnp.float32
    dma = pltpu.SemaphoreType.DMA
    return pl.pallas_call(
        functools.partial(kernel, n_ctx),
        out_shape=(
            jax.ShapeDtypeStruct((channels, block), bf16),
            jax.ShapeDtypeStruct((width, length), bf16),
        ),
        in_specs=[pl.BlockSpec(memory_space=pl.ANY)] * 4,
        out_specs=[pl.BlockSpec(memory_space=pltpu.VMEM)] * 2,
        scratch_shapes=[
            pltpu.VMEM((6, width, STEP), bf16),
            pltpu.VMEM((6, width, STEP), bf16),
            pltpu.VMEM((TAPS, width, 256), bf16),
            pltpu.VMEM((4, channels, 4 * width), bf16),
            pltpu.VMEM((channels, block), bf16),
            pltpu.VMEM((block, channels), bf16),
            pltpu.VMEM((4, width, STEP), f32),
            pltpu.VMEM((16, width, block), bf16),
            pltpu.VMEM((channels, block), bf16),
            pltpu.VMEM((16, width, block), bf16),
            pltpu.VMEM((16, width, block), bf16),
            pltpu.VMEM((channels, block), f32),
            dma((10,)),
            dma((4,)),
            dma((4,)),
            dma((16,)),
            dma((16,)),
            dma((16,)),
            dma((16,)),
        ],
        compiler_params=pltpu.CompilerParams(
            collective_id=0, has_side_effects=True, vmem_limit_bytes=40 * 1024 * 1024
        ),
        name="conv_mix_grad",
    )(*(
        pltpu.with_memory_space_constraint(a, pltpu.HBM)
        for a in (inputs, jnp.transpose(conv_weight, (0, 2, 1)), pw_weight, cotangent)
    ))


def solution(mesh):
    return jax.shard_map(
        functools.partial(body, mesh.shape["ctx"]),
        mesh=mesh,
        in_specs=(P("ch", "ctx"), P(), P(), P(None, ("ctx", "ch"))),
        out_specs=(P(None, ("ctx", "ch")), P("ch", "ctx")),
        check_vma=False,
    )
```

```python
import functools

import jax
import jax.numpy as jnp
from jax import lax
from jax.experimental import pallas as pl
from jax.experimental.pallas import tpu as pltpu
from jax.sharding import PartitionSpec as P

STEP = 512
TAPS = 3
CUBIC = 0.044715
SCALE = 0.7978845608028654
NT = (((1,), (1,)), ((), ()))


def gelu_and_slope(v):
    square = v * v
    t = jnp.tanh(SCALE * v * (1.0 + CUBIC * square))
    half = 0.5 * (1.0 + t)
    slope = half + 0.5 * v * (1.0 - t * t) * (SCALE * (1.0 + 3.0 * CUBIC * square))
    return v * half, slope


def kernel(
    n_ctx, x_hbm, wt_hbm, pw_hbm, cot_hbm, mixed_ref, gin_ref,
    xc, gc, wwin, pw_v, cot_v, cot_t, slope, act_send, act_recv, ga_send, ga_recv, total, w_cat, wt_cat,
    load_sem, halo_send, halo_recv, act_ssem, act_rsem, ga_ssem, ga_rsem,
):
    width, block = act_send.shape[1:]
    quads = 4
    me_ctx, me = lax.axis_index("ctx"), lax.axis_index("ch")
    y, x, core = me // 4, (me // 2) % 2, me % 2
    wide = quads * width

    barrier = pltpu.get_barrier_semaphore()
    has_left, has_right = me_ctx > 0, me_ctx < n_ctx - 1
    seam = n_ctx // 2 - 1
    for k in range(1, 16):
        pl.semaphore_signal(barrier, inc=1, device_id={"ch": lax.rem(me + k, 16)})

    @pl.when(has_left)
    def _():
        pl.semaphore_signal(barrier, inc=1, device_id={"ctx": me_ctx - 1})

    @pl.when(has_right)
    def _():
        pl.semaphore_signal(barrier, inc=1, device_id={"ctx": me_ctx + 1})

    cot_load = pltpu.make_async_copy(cot_hbm, cot_v, load_sem.at[5])
    cot_load.start()
    order = (1, 3, 2, 0)
    pw_loads = []

    def load_pw(n):
        at = pl.multiple_of(lax.rem(y + order[n], 4) * wide, 128)
        pw_loads.append(
            pltpu.make_async_copy(pw_hbm.at[:, pl.ds(at, wide)], pw_v.at[n], load_sem.at[6 + n])
        )
        pw_loads[-1].start()

    load_pw(0)
    start = jnp.minimum((width * me) // 128, (16 * width) // 128 - 2) * 128
    off = width * me - start
    w_load = pltpu.make_async_copy(
        wt_hbm.at[:, :, pl.ds(pl.multiple_of(start, 128), 256)], wwin, load_sem.at[0]
    )
    w_load.start()
    x_loads = []
    for q in range(4):
        x_loads.append(
            pltpu.make_async_copy(x_hbm.at[:, pl.ds(STEP * q, STEP)], xc.at[q + 1], load_sem.at[1 + q])
        )
        x_loads[-1].start()
    for n in range(1, 4):
        load_pw(n)

    def halo(buffer, side, base):
        return pltpu.make_async_remote_copy(
            src_ref=buffer.at[1 if side == 0 else 4],
            dst_ref=buffer.at[5 if side == 0 else 0],
            send_sem=halo_send.at[base + side],
            recv_sem=halo_recv.at[base + side],
            device_id={"ctx": me_ctx - 1 if side == 0 else me_ctx + 1},
        )

    cot_load.wait()
    cot_t[...] = cot_v[...].T

    def grad_active(n):
        pw_loads[n].wait()
        flipped = jnp.dot(cot_t[...], pw_v[n], preferred_element_type=jnp.float32).T.astype(jnp.bfloat16)
        for b in range(4):
            ga_send[4 * n + b] = flipped[width * b : width * (b + 1), :]

    def send_ga(n):
        dy = order[n]
        for k, (dx, dc) in enumerate(((1, 0), (1, 1), (0, 1), (0, 0))):
            low = 2 * lax.rem(x + dx, 2) + lax.rem(core + dc, 2)
            if dy or dx or dc:
                pltpu.make_async_remote_copy(
                    src_ref=ga_send.at[4 * n + low],
                    dst_ref=ga_recv.at[me],
                    send_sem=ga_ssem.at[4 * n + k],
                    recv_sem=ga_rsem.at[me],
                    device_id={"ch": 4 * lax.rem(y + dy, 4) + low},
                ).start()
            else:
                pltpu.make_async_copy(ga_send.at[4 * n + low], ga_recv.at[me], ga_rsem.at[me]).start()

    def conv(q):
        signal = jnp.concatenate([xc[q], xc[q + 1], xc[q + 2]], axis=0)
        act, tilt = gelu_and_slope(jnp.dot(w_cat[...], signal, preferred_element_type=jnp.float32))
        slope[q] = tilt
        act = act.astype(jnp.bfloat16)
        for b in range(4):
            act_send[4 * q + b] = act[:, block * b : block * (b + 1)]

    def send_act(q):
        for n, (dx, dc) in enumerate(((1, 0), (1, 1), (0, 1), (0, 0))):
            to = 4 * q + 2 * lax.rem(x + dx, 2) + lax.rem(core + dc, 2)
            copy = pltpu.make_async_remote_copy(
                src_ref=act_send.at[to],
                dst_ref=act_recv.at[pl.ds(pl.multiple_of(width * me, width), width), :],
                send_sem=act_ssem.at[4 * q + n],
                recv_sem=act_rsem.at[me],
                device_id={"ch": to},
            )
            if dx or dc:
                copy.start()
            else:
                pl.when(y != q)(copy.start)

                @pl.when(y == q)
                def _():
                    pltpu.make_async_copy(
                        act_send.at[to],
                        act_recv.at[pl.ds(pl.multiple_of(width * me, width), width), :],
                        act_rsem.at[me],
                    ).start()

    def wait_sent(q_sems, buffer):
        pltpu.make_async_copy(buffer, buffer, q_sems).wait()

    def kernel_taps():
        w_load.wait()
        rows = lax.broadcasted_iota(jnp.int32, (width, 256), 0)
        lanes = lax.broadcasted_iota(jnp.int32, (width, 256), 1)
        pick = jnp.where(lanes == rows + off, 1.0, 0.0).astype(jnp.bfloat16)
        w = lax.dot_general(
            pick, wwin[...].reshape(TAPS * width, 256), NT, preferred_element_type=jnp.float32
        )
        w_cat[...] = w.astype(jnp.bfloat16)
        depth = lax.broadcasted_iota(jnp.int32, (256, TAPS * width), 0)
        column = lax.broadcasted_iota(jnp.int32, (256, TAPS * width), 1)
        wt = jnp.zeros((width, TAPS * width), jnp.float32)
        for t in range(TAPS):
            hit = (depth == column - width * t + off) & (column >= width * t) & (column < width * (t + 1))
            place = jnp.where(hit, 1.0, 0.0).astype(jnp.bfloat16)
            wt = wt + jnp.dot(wwin[t], place, preferred_element_type=jnp.float32)
        wt_cat[...] = wt.astype(jnp.bfloat16)

    early = (lax.rem(me_ctx, n_ctx // 2) == 0) & (me_ctx + me > 0)
    grad_active(0)
    for q in range(4):
        x_loads[q].wait()

    @pl.when(early)
    def _():
        for n in range(1, 4):
            grad_active(n)
        kernel_taps()
        conv(1)
        conv(2)

    pl.semaphore_wait(barrier, 15 + has_left.astype(jnp.int32) + has_right.astype(jnp.int32))
    pl.when(has_right)(lambda: halo(xc, 1, 0).start())
    pl.when(has_left)(lambda: halo(xc, 0, 0).start())
    send_ga(0)

    @pl.when(early)
    def _():
        for n in range(1, 4):
            send_ga(n)
        send_act(1)
        send_act(2)

    @pl.when(jnp.logical_not(early))
    def _():
        for n in range(1, 4):
            grad_active(n)
            send_ga(n)
        kernel_taps()
        conv(1)
        send_act(1)
        conv(2)
        send_act(2)

    @pl.when(has_left)
    def _():
        halo(xc, 1, 0).wait_recv()

    @pl.when(jnp.logical_not(has_left))
    def _():
        xc[0] = jnp.zeros(xc.shape[1:], xc.dtype)

    conv(0)
    pl.when(me_ctx != seam)(lambda: send_act(0))

    @pl.when(has_right)
    def _():
        halo(xc, 0, 0).wait_recv()

    @pl.when(jnp.logical_not(has_right))
    def _():
        xc[5] = jnp.zeros(xc.shape[1:], xc.dtype)

    conv(3)
    pl.when(me_ctx != seam)(lambda: send_act(3))

    def grad_conv(q):
        for b in range(4):
            s = 4 * q + b
            pltpu.make_async_copy(ga_recv.at[s], ga_recv.at[s], ga_rsem.at[s]).wait()
            gc[q + 1, :, pl.ds(block * b, block)] = (
                ga_recv[s].astype(jnp.float32) * slope[q, :, pl.ds(block * b, block)]
            ).astype(jnp.bfloat16)

    grad_conv(3)
    pl.when(has_right)(lambda: halo(gc, 1, 2).start())
    grad_conv(0)
    pl.when(has_left)(lambda: halo(gc, 0, 2).start())

    @pl.when(me_ctx == seam)
    def _():
        send_act(0)
        send_act(3)

    grad_conv(1)
    grad_conv(2)

    def back(q):
        signal = jnp.concatenate([gc[q + 2], gc[q + 1], gc[q]], axis=0)
        gin_ref[:, pl.ds(STEP * q, STEP)] = jnp.dot(
            wt_cat[...], signal, preferred_element_type=jnp.float32
        ).astype(jnp.bfloat16)

    back(1)
    back(2)

    visit = (3, 0, 1, 2)

    def mix(k):
        n = visit[k]
        from_y = lax.rem(y + order[n], 4)
        for b in range(4):
            s = 4 * from_y + b
            piece = act_recv.at[pl.ds(pl.multiple_of(width * s, width), width), :]
            pltpu.make_async_copy(piece, piece, act_rsem.at[s]).wait()
        part = jnp.dot(
            pw_v[n],
            act_recv[pl.ds(pl.multiple_of(wide * from_y, wide), wide), :],
            preferred_element_type=jnp.float32,
        )
        if k == 0:
            total[...] = part
        elif k < 3:
            total[...] += part
        else:
            mixed_ref[...] = (total[...] + part).astype(jnp.bfloat16)

    for k in range(3):
        mix(k)

    @pl.when(has_right)
    def _():
        halo(gc, 0, 2).wait_recv()

    @pl.when(jnp.logical_not(has_right))
    def _():
        gc[5] = jnp.zeros(gc.shape[1:], gc.dtype)

    back(3)
    mix(3)

    @pl.when(has_left)
    def _():
        halo(gc, 1, 2).wait_recv()

    @pl.when(jnp.logical_not(has_left))
    def _():
        gc[0] = jnp.zeros(gc.shape[1:], gc.dtype)

    back(0)

    for q in range(4):
        for n in range(4):
            if n < 3:
                wait_sent(act_ssem.at[4 * q + n], act_send.at[0])
            else:
                pl.when(y != q)(lambda: wait_sent(act_ssem.at[4 * q + n], act_send.at[0]))
            if order[q] or n < 3:
                wait_sent(ga_ssem.at[4 * q + n], ga_send.at[0])
    for base, buffer in ((0, xc), (2, gc)):
        pl.when(has_left)(lambda: halo(buffer, 0, base).wait_send())
        pl.when(has_right)(lambda: halo(buffer, 1, base).wait_send())


def write_out(mixed_ref, gin_ref, mixed_hbm, gin_hbm, sem):
    copies = (
        pltpu.make_async_copy(mixed_ref, mixed_hbm, sem.at[0]),
        pltpu.make_async_copy(gin_ref, gin_hbm, sem.at[1]),
    )
    for copy in copies:
        copy.start()
    for copy in copies:
        copy.wait()


def body(n_ctx, inputs, conv_weight, pw_weight, cotangent):
    width, length = inputs.shape
    channels, block = cotangent.shape
    bf16, f32 = jnp.bfloat16, jnp.float32
    dma = pltpu.SemaphoreType.DMA
    mixed, grad_inputs = pl.pallas_call(
        functools.partial(kernel, n_ctx),
        out_shape=(
            jax.ShapeDtypeStruct((channels, block), bf16),
            jax.ShapeDtypeStruct((width, length), bf16),
        ),
        in_specs=[pl.BlockSpec(memory_space=pl.ANY)] * 4,
        out_specs=[pl.BlockSpec(memory_space=pltpu.VMEM)] * 2,
        scratch_shapes=[
            pltpu.VMEM((6, width, STEP), bf16),
            pltpu.VMEM((6, width, STEP), bf16),
            pltpu.VMEM((TAPS, width, 256), bf16),
            pltpu.VMEM((4, channels, 4 * width), bf16),
            pltpu.VMEM((channels, block), bf16),
            pltpu.VMEM((block, channels), bf16),
            pltpu.VMEM((4, width, STEP), f32),
            pltpu.VMEM((16, width, block), bf16),
            pltpu.VMEM((channels, block), bf16),
            pltpu.VMEM((16, width, block), bf16),
            pltpu.VMEM((16, width, block), bf16),
            pltpu.VMEM((channels, block), f32),
            pltpu.VMEM((width, TAPS * width), bf16),
            pltpu.VMEM((width, TAPS * width), bf16),
            dma((10,)),
            dma((4,)),
            dma((4,)),
            dma((16,)),
            dma((16,)),
            dma((16,)),
            dma((16,)),
        ],
        compiler_params=pltpu.CompilerParams(
            collective_id=0, has_side_effects=True, vmem_limit_bytes=40 * 1024 * 1024
        ),
        name="conv_mix_grad",
    )(*(
        pltpu.with_memory_space_constraint(a, pltpu.HBM)
        for a in (inputs, jnp.transpose(conv_weight, (0, 2, 1)), pw_weight, cotangent)
    ))
    return pl.pallas_call(
        write_out,
        out_shape=(
            jax.ShapeDtypeStruct(mixed.shape, bf16),
            jax.ShapeDtypeStruct(grad_inputs.shape, bf16),
        ),
        in_specs=[pl.BlockSpec(memory_space=pl.ANY)] * 2,
        out_specs=[pl.BlockSpec(memory_space=pltpu.HBM)] * 2,
        scratch_shapes=[dma((2,))],
        compiler_params=pltpu.CompilerParams(vmem_limit_bytes=4 * 1024 * 1024),
        name="write_out",
    )(mixed, grad_inputs)


def solution(mesh):
    return jax.shard_map(
        functools.partial(body, mesh.shape["ctx"]),
        mesh=mesh,
        in_specs=(P("ch", "ctx"), P(), P(), P(None, ("ctx", "ch"))),
        out_specs=(P(None, ("ctx", "ch")), P("ch", "ctx")),
        check_vma=False,
    )
```

```python
import functools

import jax
import jax.numpy as jnp
from jax import lax
from jax.experimental import pallas as pl
from jax.experimental.pallas import tpu as pltpu
from jax.sharding import PartitionSpec as P

STEP = 512
TAPS = 3
CUBIC = 0.044715
SCALE = 0.7978845608028654
NT = (((1,), (1,)), ((), ()))


def gelu_and_slope(v):
    square = v * v
    t = jnp.tanh(SCALE * v * (1.0 + CUBIC * square))
    half = 0.5 * (1.0 + t)
    slope = half + 0.5 * v * (1.0 - t * t) * (SCALE * (1.0 + 3.0 * CUBIC * square))
    return v * half, slope


def kernel(
    n_ctx, x_hbm, wt_hbm, pw_hbm, cot_hbm, mixed_ref, gin_ref,
    xc, gc, wwin, pw_v, cot_v, cot_t, slope, act_send, act_recv, ga_send, ga_recv, total, w_cat, wt_cat,
    load_sem, halo_send, halo_recv, act_ssem, act_rsem, ga_ssem, ga_rsem,
):
    width, block = act_send.shape[1:]
    quads = 4
    me_ctx, me = lax.axis_index("ctx"), lax.axis_index("ch")
    y, x, core = me // 4, (me // 2) % 2, me % 2
    wide = quads * width

    barrier = pltpu.get_barrier_semaphore()
    has_left, has_right = me_ctx > 0, me_ctx < n_ctx - 1
    seam = n_ctx // 2 - 1
    for k in range(1, 16):
        pl.semaphore_signal(barrier, inc=1, device_id={"ch": lax.rem(me + k, 16)})

    @pl.when(has_left)
    def _():
        pl.semaphore_signal(barrier, inc=1, device_id={"ctx": me_ctx - 1})

    @pl.when(has_right)
    def _():
        pl.semaphore_signal(barrier, inc=1, device_id={"ctx": me_ctx + 1})

    cot_load = pltpu.make_async_copy(cot_hbm, cot_v, load_sem.at[5])
    cot_load.start()
    order = (2, 1, 3, 0)
    pw_loads = []

    def load_pw(n):
        at = pl.multiple_of(lax.rem(y + order[n], 4) * wide, 128)
        pw_loads.append(
            pltpu.make_async_copy(pw_hbm.at[:, pl.ds(at, wide)], pw_v.at[n], load_sem.at[6 + n])
        )
        pw_loads[-1].start()

    load_pw(0)
    start = jnp.minimum((width * me) // 128, (16 * width) // 128 - 2) * 128
    off = width * me - start
    w_load = pltpu.make_async_copy(
        wt_hbm.at[:, :, pl.ds(pl.multiple_of(start, 128), 256)], wwin, load_sem.at[0]
    )
    w_load.start()
    x_loads = []
    for q in range(4):
        x_loads.append(
            pltpu.make_async_copy(x_hbm.at[:, pl.ds(STEP * q, STEP)], xc.at[q + 1], load_sem.at[1 + q])
        )
        x_loads[-1].start()
    for n in range(1, 4):
        load_pw(n)

    def halo(buffer, side, base):
        return pltpu.make_async_remote_copy(
            src_ref=buffer.at[1 if side == 0 else 4],
            dst_ref=buffer.at[5 if side == 0 else 0],
            send_sem=halo_send.at[base + side],
            recv_sem=halo_recv.at[base + side],
            device_id={"ctx": me_ctx - 1 if side == 0 else me_ctx + 1},
        )

    cot_load.wait()
    cot_t[...] = cot_v[...].T

    def grad_active(n):
        pw_loads[n].wait()
        flipped = jnp.dot(cot_t[...], pw_v[n], preferred_element_type=jnp.float32).T.astype(jnp.bfloat16)
        for b in range(4):
            ga_send[4 * n + b] = flipped[width * b : width * (b + 1), :]

    def send_ga(n):
        dy = order[n]
        for k, (dx, dc) in enumerate(((1, 0), (1, 1), (0, 1), (0, 0))):
            low = 2 * lax.rem(x + dx, 2) + lax.rem(core + dc, 2)
            if dy or dx or dc:
                pltpu.make_async_remote_copy(
                    src_ref=ga_send.at[4 * n + low],
                    dst_ref=ga_recv.at[me],
                    send_sem=ga_ssem.at[4 * n + k],
                    recv_sem=ga_rsem.at[me],
                    device_id={"ch": 4 * lax.rem(y + dy, 4) + low},
                ).start()
            else:
                pltpu.make_async_copy(ga_send.at[4 * n + low], ga_recv.at[me], ga_rsem.at[me]).start()

    def conv(q):
        signal = jnp.concatenate([xc[q], xc[q + 1], xc[q + 2]], axis=0)
        act, tilt = gelu_and_slope(jnp.dot(w_cat[...], signal, preferred_element_type=jnp.float32))
        slope[q] = tilt
        act = act.astype(jnp.bfloat16)
        for b in range(4):
            act_send[4 * q + b] = act[:, block * b : block * (b + 1)]

    def send_act(q):
        for n, (dx, dc) in enumerate(((1, 0), (1, 1), (0, 1), (0, 0))):
            to = 4 * q + 2 * lax.rem(x + dx, 2) + lax.rem(core + dc, 2)
            copy = pltpu.make_async_remote_copy(
                src_ref=act_send.at[to],
                dst_ref=act_recv.at[pl.ds(pl.multiple_of(width * me, width), width), :],
                send_sem=act_ssem.at[4 * q + n],
                recv_sem=act_rsem.at[me],
                device_id={"ch": to},
            )
            if dx or dc:
                copy.start()
            else:
                pl.when(y != q)(copy.start)

                @pl.when(y == q)
                def _():
                    pltpu.make_async_copy(
                        act_send.at[to],
                        act_recv.at[pl.ds(pl.multiple_of(width * me, width), width), :],
                        act_rsem.at[me],
                    ).start()

    def wait_sent(q_sems, buffer):
        pltpu.make_async_copy(buffer, buffer, q_sems).wait()

    def kernel_taps():
        w_load.wait()
        rows = lax.broadcasted_iota(jnp.int32, (width, 256), 0)
        lanes = lax.broadcasted_iota(jnp.int32, (width, 256), 1)
        pick = jnp.where(lanes == rows + off, 1.0, 0.0).astype(jnp.bfloat16)
        w = lax.dot_general(
            pick, wwin[...].reshape(TAPS * width, 256), NT, preferred_element_type=jnp.float32
        )
        w_cat[...] = w.astype(jnp.bfloat16)
        depth = lax.broadcasted_iota(jnp.int32, (256, TAPS * width), 0)
        column = lax.broadcasted_iota(jnp.int32, (256, TAPS * width), 1)
        wt = jnp.zeros((width, TAPS * width), jnp.float32)
        for t in range(TAPS):
            hit = (depth == column - width * t + off) & (column >= width * t) & (column < width * (t + 1))
            place = jnp.where(hit, 1.0, 0.0).astype(jnp.bfloat16)
            wt = wt + jnp.dot(wwin[t], place, preferred_element_type=jnp.float32)
        wt_cat[...] = wt.astype(jnp.bfloat16)

    early = (lax.rem(me_ctx, n_ctx // 2) == 0) & (me_ctx + me > 0)
    grad_active(0)
    for q in range(4):
        x_loads[q].wait()

    @pl.when(early)
    def _():
        for n in range(1, 4):
            grad_active(n)
        kernel_taps()
        conv(1)
        conv(2)

    pl.semaphore_wait(barrier, 15 + has_left.astype(jnp.int32) + has_right.astype(jnp.int32))
    pl.when(has_right)(lambda: halo(xc, 1, 0).start())
    pl.when(has_left)(lambda: halo(xc, 0, 0).start())
    send_ga(0)

    @pl.when(early)
    def _():
        for n in range(1, 4):
            send_ga(n)
        send_act(1)
        send_act(2)

    @pl.when(jnp.logical_not(early))
    def _():
        for n in range(1, 4):
            grad_active(n)
            send_ga(n)
        kernel_taps()
        conv(1)
        pl.when(me_ctx != seam)(lambda: send_act(1))
        conv(2)
        pl.when(me_ctx != seam)(lambda: send_act(2))

    @pl.when(has_left)
    def _():
        halo(xc, 1, 0).wait_recv()

    @pl.when(jnp.logical_not(has_left))
    def _():
        xc[0] = jnp.zeros(xc.shape[1:], xc.dtype)

    conv(0)
    pl.when(me_ctx != seam)(lambda: send_act(0))

    @pl.when(has_right)
    def _():
        halo(xc, 0, 0).wait_recv()

    @pl.when(jnp.logical_not(has_right))
    def _():
        xc[5] = jnp.zeros(xc.shape[1:], xc.dtype)

    conv(3)
    pl.when(me_ctx != seam)(lambda: send_act(3))

    def grad_conv(q):
        for b in range(4):
            s = 4 * q + b
            pltpu.make_async_copy(ga_recv.at[s], ga_recv.at[s], ga_rsem.at[s]).wait()
            gc[q + 1, :, pl.ds(block * b, block)] = (
                ga_recv[s].astype(jnp.float32) * slope[q, :, pl.ds(block * b, block)]
            ).astype(jnp.bfloat16)

    grad_conv(3)
    pl.when(has_right)(lambda: halo(gc, 1, 2).start())
    grad_conv(0)
    pl.when(has_left)(lambda: halo(gc, 0, 2).start())

    @pl.when(me_ctx == seam)
    def _():
        for q in range(4):
            send_act(q)

    grad_conv(1)
    grad_conv(2)

    def back(q):
        signal = jnp.concatenate([gc[q + 2], gc[q + 1], gc[q]], axis=0)
        gin_ref[:, pl.ds(STEP * q, STEP)] = jnp.dot(
            wt_cat[...], signal, preferred_element_type=jnp.float32
        ).astype(jnp.bfloat16)

    back(1)
    back(2)

    visit = (3, 1, 2, 0)

    def mix(k):
        n = visit[k]
        from_y = lax.rem(y + order[n], 4)
        for b in range(4):
            s = 4 * from_y + b
            piece = act_recv.at[pl.ds(pl.multiple_of(width * s, width), width), :]
            pltpu.make_async_copy(piece, piece, act_rsem.at[s]).wait()
        part = jnp.dot(
            pw_v[n],
            act_recv[pl.ds(pl.multiple_of(wide * from_y, wide), wide), :],
            preferred_element_type=jnp.float32,
        )
        if k == 0:
            total[...] = part
        elif k < 3:
            total[...] += part
        else:
            mixed_ref[...] = (total[...] + part).astype(jnp.bfloat16)

    for k in range(3):
        mix(k)

    @pl.when(has_right)
    def _():
        halo(gc, 0, 2).wait_recv()

    @pl.when(jnp.logical_not(has_right))
    def _():
        gc[5] = jnp.zeros(gc.shape[1:], gc.dtype)

    back(3)
    mix(3)

    @pl.when(has_left)
    def _():
        halo(gc, 1, 2).wait_recv()

    @pl.when(jnp.logical_not(has_left))
    def _():
        gc[0] = jnp.zeros(gc.shape[1:], gc.dtype)

    back(0)

    for q in range(4):
        for n in range(4):
            if n < 3:
                wait_sent(act_ssem.at[4 * q + n], act_send.at[0])
            else:
                pl.when(y != q)(lambda: wait_sent(act_ssem.at[4 * q + n], act_send.at[0]))
            if order[q] or n < 3:
                wait_sent(ga_ssem.at[4 * q + n], ga_send.at[0])
    for base, buffer in ((0, xc), (2, gc)):
        pl.when(has_left)(lambda: halo(buffer, 0, base).wait_send())
        pl.when(has_right)(lambda: halo(buffer, 1, base).wait_send())


def write_out(mixed_ref, gin_ref, mixed_hbm, gin_hbm, sem):
    copies = (
        pltpu.make_async_copy(mixed_ref, mixed_hbm, sem.at[0]),
        pltpu.make_async_copy(gin_ref, gin_hbm, sem.at[1]),
    )
    for copy in copies:
        copy.start()
    for copy in copies:
        copy.wait()


def body(n_ctx, inputs, conv_weight, pw_weight, cotangent):
    width, length = inputs.shape
    channels, block = cotangent.shape
    bf16, f32 = jnp.bfloat16, jnp.float32
    dma = pltpu.SemaphoreType.DMA
    mixed, grad_inputs = pl.pallas_call(
        functools.partial(kernel, n_ctx),
        out_shape=(
            jax.ShapeDtypeStruct((channels, block), bf16),
            jax.ShapeDtypeStruct((width, length), bf16),
        ),
        in_specs=[pl.BlockSpec(memory_space=pl.ANY)] * 4,
        out_specs=[pl.BlockSpec(memory_space=pltpu.VMEM)] * 2,
        scratch_shapes=[
            pltpu.VMEM((6, width, STEP), bf16),
            pltpu.VMEM((6, width, STEP), bf16),
            pltpu.VMEM((TAPS, width, 256), bf16),
            pltpu.VMEM((4, channels, 4 * width), bf16),
            pltpu.VMEM((channels, block), bf16),
            pltpu.VMEM((block, channels), bf16),
            pltpu.VMEM((4, width, STEP), f32),
            pltpu.VMEM((16, width, block), bf16),
            pltpu.VMEM((channels, block), bf16),
            pltpu.VMEM((16, width, block), bf16),
            pltpu.VMEM((16, width, block), bf16),
            pltpu.VMEM((channels, block), f32),
            pltpu.VMEM((width, TAPS * width), bf16),
            pltpu.VMEM((width, TAPS * width), bf16),
            dma((10,)),
            dma((4,)),
            dma((4,)),
            dma((16,)),
            dma((16,)),
            dma((16,)),
            dma((16,)),
        ],
        compiler_params=pltpu.CompilerParams(
            collective_id=0, has_side_effects=True, vmem_limit_bytes=40 * 1024 * 1024
        ),
        name="conv_mix_grad",
    )(*(
        pltpu.with_memory_space_constraint(a, pltpu.HBM)
        for a in (inputs, jnp.transpose(conv_weight, (0, 2, 1)), pw_weight, cotangent)
    ))
    return pl.pallas_call(
        write_out,
        out_shape=(
            jax.ShapeDtypeStruct(mixed.shape, bf16),
            jax.ShapeDtypeStruct(grad_inputs.shape, bf16),
        ),
        in_specs=[pl.BlockSpec(memory_space=pl.ANY)] * 2,
        out_specs=[pl.BlockSpec(memory_space=pltpu.HBM)] * 2,
        scratch_shapes=[dma((2,))],
        compiler_params=pltpu.CompilerParams(vmem_limit_bytes=4 * 1024 * 1024),
        name="write_out",
    )(mixed, grad_inputs)


def solution(mesh):
    return jax.shard_map(
        functools.partial(body, mesh.shape["ctx"]),
        mesh=mesh,
        in_specs=(P("ch", "ctx"), P(), P(), P(None, ("ctx", "ch"))),
        out_specs=(P(None, ("ctx", "ch")), P("ch", "ctx")),
        check_vma=False,
    )
```
